32 devices in a mesh: rows: 16 (over z, y, core), blk: 2 (over x).
Axes of the slice: x: 2, y: 2, z: 4, core: 2. Of those that a mesh axis runs over, the one named last changes fastest.
Arguments:
- covariance: float32 [2, 2048, 2048], P('blk', 'rows'), may hold values from -1 to 4, as said below
- jac_parts: bfloat16 [16, 2, 2, 2048, 128], P('rows', None, 'blk'), may hold values from -0.046875 to 0.046875
- errors: float32 [2, 128], replicated, may hold values from -24 to 24
- noise: float32 [2, 128], replicated, may hold values from 0.5 to 2
- order: int32 [2, 128], replicated, may hold values from 0 to 127, each once within a row
Outputs:
- new_covariance: float32 [2, 2048, 2048], P('blk', 'rows')
- weight_step: float32 [2, 2048], P('blk', 'rows')
The draws below stay inside these ranges and needn't reach their ends.
Inputs may be any that keep to these rules, and one draw needn't show every extreme that they name: Each row of order names every value 0 to 127 once. Every block of covariance is symmetric and positive definite: diagonal entries between 1.2 and 3.6, off-diagonal entries of size about 0.01, every eigenvalue within 1 of the diagonal's range.
All inputs are finite; a program needn't handle non-finite values.
Results may differ from the reference program's by a relative error of at most 0.0003.
Values sent between devices are 32-bit elements; how exact they have to be, the bound alone decides.
No kernel may reach another device: no remote copies, remote signals or barrier semaphores. Data moves between devices by JAX's collectives and lax.ppermute only.
A program may use at most 64 MiB of HBM per device.

```python
import math
import jax
import jax.numpy as jnp
from jax import lax

K = 2048
M = 128
UPDATES = 2
BLOCKS = 2
N_ROWS = 16


def draw_covariance(key, part):
    key_noise = jax.random.fold_in(key, 11)
    key_diag = jax.random.fold_in(key, 12)
    random_part = jax.random.normal(key_noise, (BLOCKS, K, K), jnp.float32)
    diagonal = jnp.exp(jax.random.uniform(key_diag, (BLOCKS, K), jnp.float32, jnp.log(1.2), jnp.log(3.0)))
    symmetric = 0.5 * (random_part + jnp.swapaxes(random_part, 1, 2))
    symmetric = symmetric * (0.56 / jnp.sqrt(float(K)))
    eye_mask = jnp.eye(K, dtype=jnp.float32)
    return symmetric * (1.0 - eye_mask) + diagonal[:, :, None] * eye_mask


def spiked(result, key, source, target, parts, factor):
    def block_of(dim):
        return (jnp.arange(result.shape[dim]) // (result.shape[dim] // parts)).reshape((-1,) + (1,) * (result.ndim - 1 - dim))

    near = jax.random.permutation(key, parts)[block_of(target)]
    second = (block_of(target) + parts // 2) % parts
    return jnp.where((block_of(source) == near) | (block_of(source) == second), factor * result, result)


def levels(stream_key, extent, pieces, least, high):
    def one(axis_at, shards_of):
        draws = jax.random.uniform(jax.random.fold_in(jax.random.fold_in(stream_key, 6), axis_at), (shards_of,), jnp.float32, least / len(pieces), high / len(pieces))
        return jnp.repeat(jnp.exp(draws), extent[axis_at] // shards_of).reshape((-1,) + (1,) * (len(extent) - axis_at - 1))

    gain = one(*pieces[0])
    for cut in pieces[1:]:
        gain = gain * one(*cut)
    return gain


def bell_draw(key, dims, spread, reach, shards=(), kind=jnp.bfloat16):
    drawn = jax.random.normal(key, dims, jnp.float32) * spread
    if len(shards) > 0:
        drawn = levels(key, dims, shards, -0.22, 0.18) * drawn
    return jnp.clip(drawn, min=-reach, max=reach).astype(kind)


def gaussian_with(stream_key, dims, spread, reach, split, heavy, kind=jnp.bfloat16):
    values = spread * jax.random.normal(stream_key, dims, jnp.float32)
    if split:
        values = values * levels(stream_key, dims, split, -0.22, 0.18)
    return jnp.clip(spiked(values, jax.random.fold_in(stream_key, 3), *heavy), -reach, reach).astype(kind)


def setup_inputs(seed: int = 0) -> dict:
    key_list = jax.random.split(jax.random.key(seed), 6)
    return {
        "covariance": draw_covariance(jax.random.fold_in(key_list[5], 71), 0),
        "jac_parts": gaussian_with(key_list[1], (N_ROWS, UPDATES, BLOCKS, K, M), (2.0 * (N_ROWS * BLOCKS * K) ** -0.5), 0.046875, ((0, 16), (2, 2)), (0, 3, 16, 2.0)),
        "errors": bell_draw(key_list[2], (UPDATES, M), 4.0, 24.0, (), jnp.float32),
        "noise": jnp.clip(jnp.exp(jax.random.uniform(key_list[3], (UPDATES, M), jnp.float32, math.log(0.5), math.log(2.0))), 0.5, 2.0),
        "order": jax.vmap(lambda own: jax.random.permutation(own, M))(jax.random.split(key_list[4], UPDATES)).reshape((UPDATES, M)).astype(jnp.int32),
    }


def reference(covariance, jac_parts, errors, noise, order):

    def add_worker(summed, part):
        return (summed + part.astype(jnp.float32), None)
    start_sum = jnp.zeros(jac_parts.shape[1:], jnp.float32)
    jac_sum, _ = lax.scan(add_worker, start_sum, jac_parts)
    picked_err = jnp.take_along_axis(errors, order, axis=1)
    picked_noise = jnp.take_along_axis(noise, order, axis=1)
    highest = lax.Precision.HIGHEST
    covar_now = covariance
    weight_step = jnp.zeros(covariance.shape[:2], jnp.float32)
    for update in range(UPDATES):
        jac_now = jac_sum[update]
        prod_rows = jnp.einsum('bik,bkm->bim', covar_now, jac_now, precision=highest)
        innov = jnp.einsum('bim,bin->mn', jac_now, prod_rows, precision=highest)
        innov = innov + jnp.diag(picked_noise[update])
        shifted = jnp.einsum('bim,bi->m', jac_now, weight_step, precision=highest)
        resid = picked_err[update] - shifted
        factor = jnp.linalg.cholesky(innov)
        flat = prod_rows.reshape(-1, prod_rows.shape[2])
        kalman_gain = jax.scipy.linalg.cho_solve((factor, True), flat.T).T.reshape(prod_rows.shape)
        weight_step = weight_step + jnp.einsum('bim,m->bi', kalman_gain, resid, precision=highest)
        covar_now = covar_now - jnp.einsum('bim,bjm->bij', kalman_gain, prod_rows, precision=highest)
    return (covar_now, weight_step)
```

```python
import functools

import jax
import jax.numpy as jnp
from jax import lax
from jax.experimental import pallas as pl
from jax.experimental.pallas import tpu as pltpu
from jax.sharding import PartitionSpec as P


highest = lax.Precision.HIGHEST
NN = (((1,), (0,)), ((), ()))
NT = (((1,), (1,)), ((), ()))
TN = (((0,), (0,)), ((), ()))


def dot(a, b, dims=NN):
    return lax.dot_general(a, b, dims, precision=highest, preferred_element_type=jnp.float32)


def vmem(count):
    return [pl.BlockSpec(memory_space=pltpu.VMEM)] * count


class Grid:
    def __init__(self, size):
        self.size = size
        self.cores = 2 if size % 2 == 0 else 1
        chips = size // self.cores
        self.ys = 1
        while self.ys * self.ys * 4 <= chips and chips % (self.ys * 2) == 0:
            self.ys *= 2
        self.zs = chips // self.ys

    def split(self, index):
        return index // (self.ys * self.cores), (index // self.cores) % self.ys, index % self.cores

    def join(self, z, y, core):
        return (z * self.ys + y) * self.cores + core

    def send(self, x, dz=0, dy=0, dc=0):
        pairs = []
        for source in range(self.size):
            z, y, core = self.split(source)
            target = self.join((z + dz) % self.zs, (y + dy) % self.ys, (core + dc) % self.cores)
            pairs.append((source, target))
        return lax.ppermute(x, "rows", pairs)

    def z_order(self):
        return sorted(range(1, self.zs), key=lambda k: min(k, self.zs - k))


def reduce_scatter(grid, terms):
    updates, rows, measures = terms.shape
    panel = rows // grid.size
    cut = terms.reshape(updates, grid.zs, grid.ys, grid.cores, panel, measures)
    z, y, core = grid.split(lax.axis_index("rows"))

    def own(k, j, dc):
        at = (0, (z + k) % grid.zs, (y + j) % grid.ys, (core + dc) % grid.cores, 0, 0)
        piece = lax.dynamic_slice(cut, at, (updates, 1, 1, 1, panel, measures))
        return piece.reshape(updates, panel, measures).astype(jnp.float32)

    def own_ys(k, dc):
        at = (0, (z + k) % grid.zs, 0, (core + dc) % grid.cores, 0, 0)
        piece = lax.dynamic_slice(cut, at, (updates, 1, grid.ys, 1, panel, measures))
        return piece.reshape(updates, grid.ys, panel, measures).astype(jnp.float32)

    def at_y(pieces, j):
        piece = lax.dynamic_slice_in_dim(pieces, (y + j) % grid.ys, 1, axis=1)
        return piece.reshape(updates, panel, measures)

    order = list(reversed(grid.z_order())) + [0]
    core_got = {}
    for k in order:
        core_got[k] = [grid.send(own_ys(k, dc), dc=dc) for dc in range(1, grid.cores)]
    y_got = {}
    for k in order:
        for j in range(1, grid.ys):
            term = own(k, j, 0)
            for got in core_got[k]:
                term = term + at_y(got, j)
            y_got[k, j] = grid.send(term, dy=j)
    total = None
    z_got = []
    for k in order:
        term = own(k, 0, 0)
        for got in core_got[k]:
            term = term + at_y(got, 0)
        for j in range(1, grid.ys):
            term = term + y_got[k, j]
        if k:
            z_got.append(grid.send(term, dz=k))
        else:
            total = term
    for got in z_got:
        total = total + got
    return total


def all_gather(grid, piece):
    have = {(0, 0, 0): piece}
    z_keys = [0] + grid.z_order()
    for k in z_keys[1:]:
        have[k, 0, 0] = grid.send(piece, dz=k)
    for k in z_keys:
        for j in range(1, grid.ys):
            have[k, j, 0] = grid.send(have[k, 0, 0], dy=j)
    for dc in range(1, grid.cores):
        for j in range(grid.ys):
            for k in z_keys:
                have[k, j, dc] = grid.send(have[k, j, 0], dc=dc)
    return have


def place(grid, keys, pieces, whole_ref):
    z, y, core = grid.split(lax.axis_index("rows"))
    for (k, j, dc), piece in zip(keys, pieces):
        source = grid.join(
            lax.rem(z + grid.zs - k, grid.zs),
            lax.rem(y + grid.ys - j, grid.ys),
            lax.rem(core + grid.cores - dc, grid.cores),
        )
        updates, panel, measures = piece.shape
        first = pl.multiple_of(source * panel, panel)
        for update in range(updates):
            whole_ref[pl.ds(first, panel), update * measures : (update + 1) * measures] = piece[update]


def product_kernel(grid, keys, covar_ref, *refs):
    pieces, (prod_ref, jac_ref) = refs[:-2], refs[-2:]
    place(grid, keys, pieces, jac_ref)
    measures = prod_ref.shape[2]
    prod = dot(covar_ref[...], jac_ref[...])
    for update in range(prod_ref.shape[0]):
        prod_ref[update] = prod[:, update * measures : (update + 1) * measures]


def innov_kernel(grid, keys, jac_ref, *refs):
    pieces, (corr_ref, whole_ref) = refs[:-2], refs[-2:]
    place(grid, keys, pieces, whole_ref)
    m = corr_ref.shape[2]
    both = dot(jac_ref[...], whole_ref[...], TN)
    corr_ref[0] = both[:m, :m]
    corr_ref[1] = both[m:, :m]
    corr_ref[2] = both[m:, m:]


def pick_kernel(errors_ref, noise_ref, order_ref, picked_ref):
    updates, measures = errors_ref.shape
    entry = lax.broadcasted_iota(jnp.int32, (measures, measures), 0)
    for update in range(updates):
        chosen = (entry == order_ref[update : update + 1, :]).astype(jnp.float32)
        picked_ref[update : update + 1, :] = dot(errors_ref[update : update + 1, :], chosen)
        picked_ref[updates + update : updates + update + 1, :] = dot(noise_ref[update : update + 1, :], chosen)


def invert(matrix, step=2):
    size = matrix.shape[0]
    lane = lax.broadcasted_iota(jnp.int32, (1, size), 1)
    sub = lax.broadcasted_iota(jnp.int32, (8, 1), 0)
    for at in range(0, size, 2):
        a = matrix[at : at + 1, at : at + 1]
        b = matrix[at + 1 : at + 2, at : at + 1]
        d = matrix[at + 1 : at + 2, at + 1 : at + 2]
        inv = 1.0 / (a * d - b * b)
        col0 = matrix[:, at : at + 1]
        col1 = matrix[:, at + 1 : at + 2]
        is0 = lane == at
        is1 = lane == at + 1
        clear = is0 | is1
        row0 = jnp.where(is0, 1.0, jnp.where(is1, 0.0, matrix[at : at + 1, :]))
        row1 = jnp.where(is1, 1.0, jnp.where(is0, 0.0, matrix[at + 1 : at + 2, :]))
        new0 = (d * inv) * row0 - (b * inv) * row1
        new1 = (a * inv) * row1 - (b * inv) * row0
        base = at // 8 * 8
        parts = []
        if base:
            parts.append(jnp.where(clear, 0.0, matrix[:base]) - col0[:base] * new0 - col1[:base] * new1)
        mid = slice(base, base + 8)
        part = jnp.where(clear, 0.0, matrix[mid]) - col0[mid] * new0 - col1[mid] * new1
        part = jnp.where(sub == at - base, new0, jnp.where(sub == at - base + 1, new1, part))
        parts.append(part)
        if base + 8 < size:
            parts.append(jnp.where(clear, 0.0, matrix[base + 8 :]) - col0[base + 8 :] * new0 - col1[base + 8 :] * new1)
        matrix = jnp.concatenate(parts, axis=0) if len(parts) > 1 else parts[0]
    return matrix


def update_kernel(picked_ref, covar_ref, prod_ref, whole_ref, *refs):
    corrs, (out_ref, step_ref) = refs[:-2], refs[-2:]
    m = prod_ref.shape[2]
    diagonal = lax.broadcasted_iota(jnp.int32, (m, m), 0) == lax.broadcasted_iota(jnp.int32, (m, m), 1)

    def summed(which):
        total = corrs[0][which]
        for corr in corrs[1:]:
            total = total + corr[which]
        return total

    err0, err1 = picked_ref[0:1, :], picked_ref[1:2, :]
    inv0 = invert(summed(0) + jnp.where(diagonal, picked_ref[2:3, :], 0.0))
    step0 = dot(err0, inv0)
    resid1 = err1 - dot(step0, summed(1), NT)
    innov1 = summed(2) + jnp.where(diagonal, picked_ref[3:4, :], 0.0)
    mixed = None
    for corr in corrs:
        ratio = dot(corr[1], inv0)
        mixed = ratio if mixed is None else mixed
        innov1 = innov1 - dot(ratio, corr[1], NT)
    inv1 = invert(innov1)
    step1 = dot(resid1, inv1)
    prod0 = prod_ref[0]
    prod1 = prod_ref[1] - dot(prod0, mixed, NT)
    step_ref[...] = dot(step0, prod0, NT) + dot(step1, prod1, NT)
    gain1 = dot(prod1, inv1)
    gain0 = dot(prod0, inv0) - dot(gain1, mixed)
    gain = jnp.concatenate([gain0, gain1], axis=1)
    out_ref[...] = covar_ref[...] - dot(gain, whole_ref[...], NT)


def body(sizes, covariance, jac_parts, errors, noise, order):
    blocks = sizes["blk"]
    grid = Grid(sizes["rows"])
    _, panel, size = covariance.shape
    updates, measures = errors.shape
    covar = covariance.reshape(panel, size)
    f32 = lambda *shape: jax.ShapeDtypeStruct(shape, jnp.float32)

    picked = pl.pallas_call(
        pick_kernel, out_shape=f32(2 * updates, measures), in_specs=vmem(3), out_specs=vmem(1)[0]
    )(errors, noise, order)
    jac_own = reduce_scatter(grid, jac_parts.reshape(updates, size, measures))
    jacs = all_gather(grid, jac_own)
    keys = list(jacs)
    prod_own, jac = pl.pallas_call(
        functools.partial(product_kernel, grid, keys),
        out_shape=(f32(updates, panel, measures), f32(size, updates * measures)),
        in_specs=vmem(1 + len(keys)),
        out_specs=tuple(vmem(2)),
    )(covar, *jacs.values())
    prods = all_gather(grid, prod_own)
    corr, prod = pl.pallas_call(
        functools.partial(innov_kernel, grid, keys),
        out_shape=(f32(3, measures, measures), f32(size, updates * measures)),
        in_specs=vmem(1 + len(keys)),
        out_specs=tuple(vmem(2)),
    )(jac, *prods.values())
    corrs = [corr] + [
        lax.ppermute(corr, "blk", [(b, (b + shift) % blocks) for b in range(blocks)]) for shift in range(1, blocks)
    ]
    out, step = pl.pallas_call(
        update_kernel,
        out_shape=(f32(panel, size), f32(1, panel)),
        in_specs=vmem(4 + blocks),
        out_specs=tuple(vmem(2)),
    )(picked, covar, prod_own, prod, *corrs)
    return out.reshape(covariance.shape), step


def solution(mesh):
    in_specs = (P("blk", "rows", None), P("rows", None, "blk", None, None), P(), P(), P())
    out_specs = (P("blk", "rows", None), P("blk", "rows"))
    sizes = dict(mesh.shape)
    return jax.shard_map(
        functools.partial(body, sizes), mesh=mesh, in_specs=in_specs, out_specs=out_specs, check_vma=False
    )
```

```python
import functools
import math

import jax
import jax.numpy as jnp
from jax import lax
from jax.experimental import pallas as pl
from jax.experimental.pallas import tpu as pltpu
from jax.sharding import PartitionSpec as P


NN = (((1,), (0,)), ((), ()))
NT = (((1,), (1,)), ((), ()))
f32, bf16 = jnp.float32, jnp.bfloat16


def shape(*dims, dtype=f32):
    return jax.ShapeDtypeStruct(dims, dtype)


def call(kernel, outs, *args, anywhere=(), scratch=(), flops=0, room=8 << 20):
    space = lambda i: pl.ANY if i in anywhere else pltpu.VMEM
    moved = sum(math.prod(x.shape) * x.dtype.itemsize for x in args + tuple(outs))
    return pl.pallas_call(
        kernel,
        out_shape=tuple(outs),
        in_specs=[pl.BlockSpec(memory_space=space(i)) for i in range(len(args))],
        out_specs=tuple(pl.BlockSpec(memory_space=pltpu.VMEM) for _ in outs),
        scratch_shapes=list(scratch),
        cost_estimate=pl.CostEstimate(flops=flops, bytes_accessed=moved, transcendentals=0),
        compiler_params=pltpu.CompilerParams(vmem_limit_bytes=moved + room),
    )(*args)


def halves(x):
    high = x.astype(bf16)
    return high, (x - high.astype(f32)).astype(bf16)


def dot(a, b, dims=NN):
    return lax.dot_general(a, b, dims, precision=lax.Precision.HIGHEST, preferred_element_type=f32)


def dot_halves(a, b, dims=NN):
    mul = lambda x, y: lax.dot_general(x, y, dims, preferred_element_type=f32)
    return mul(a[0], b[0]) + (mul(a[0], b[1]) + mul(a[1], b[0]))


def dot3(a, b, dims=NN):
    return dot_halves(halves(a), halves(b), dims)


class Grid:
    def __init__(self, size):
        self.size = size
        self.cores = 2
        chips = size // self.cores
        self.ys = 1
        while self.ys * self.ys * 4 <= chips:
            self.ys *= 2
        self.zs = chips // self.ys
        self.z_order = sorted(range(1, self.zs), key=lambda k: (k % 2, k))

    def here(self):
        index = lax.axis_index("rows")
        return index // (self.ys * self.cores), (index // self.cores) % self.ys, index % self.cores

    def chip(self, k, j):
        z, y, _ = self.here()
        return (z ^ k) * self.ys + (y ^ j)

    def send(self, x, k=0, j=0, c=0):
        change = (k * self.ys + j) * self.cores + c
        return lax.ppermute(x, "rows", [(source, source ^ change) for source in range(self.size)])


def cut_kernel(grid, order, jac_ref, *refs):
    sent, kept, (buffer, sems) = refs[: len(order)], refs[len(order) : -2], refs[-2:]
    z, _, core = grid.here()
    copies = []
    for i, k in enumerate(order):
        for which, update in enumerate((1 - core, core)):
            into = buffer.at[i] if which == 0 else kept[i]
            copies.append(pltpu.make_async_copy(jac_ref.at[update, z ^ k], into, sems.at[i, which]))
            copies[-1].start()
    for i in range(len(order)):
        copies[2 * i].wait()
        sent[i][...] = buffer[i].astype(f32)
    for i in range(len(order)):
        copies[2 * i + 1].wait()


def core_sum_kernel(grid, got_ref, own_ref, *refs):
    _, y, _ = grid.here()
    for j, ref in enumerate(refs):
        ref[...] = got_ref[y ^ j] + own_ref[y ^ j].astype(f32)


def sum_kernel(count, *refs):
    refs[count][...] = tree([ref[...] for ref in refs[:count]])


def reduce_scatter(grid, terms):
    updates, rows, measures = terms.shape
    chip_rows = rows // (grid.zs * grid.ys)
    terms = terms.reshape(updates, grid.zs, grid.ys, chip_rows, measures)
    part = (grid.ys, chip_rows, measures)
    order = grid.z_order + [0]
    sent, kept = {}, {}
    for some in (order[:1], order[1:]):
        parts = call(
            functools.partial(cut_kernel, grid, some),
            [shape(*part)] * len(some) + [shape(*part, dtype=bf16)] * len(some),
            terms,
            anywhere=(0,),
            scratch=(pltpu.VMEM((len(some), *part), bf16), pltpu.SemaphoreType.DMA((len(some), 2))),
        )
        for i, k in enumerate(some):
            sent[k], kept[k] = parts[i], parts[len(some) + i]
    sums = {}
    for k in order:
        got = grid.send(sent[k], c=1)
        sums[k] = call(
            functools.partial(core_sum_kernel, grid), [shape(*part[1:])] * grid.ys, got, kept[k]
        )
    last = []
    for k in order:
        terms = [sums[k][0]] + [grid.send(sums[k][j], j=j) for j in range(1, grid.ys)]
        if k:
            total = call(functools.partial(sum_kernel, len(terms)), [shape(*part[1:])], *terms)[0]
            last.append(grid.send(total, k=k))
        else:
            last = terms + last
    return last


def all_gather(grid, piece):
    have = {(0, 0): piece}
    for j in range(1, grid.ys):
        have[0, j] = grid.send(piece, j=j)
    for k in grid.z_order:
        have[k, 0] = grid.send(piece, k=k)
    for k in grid.z_order:
        for j in range(1, grid.ys):
            have[k, j] = grid.send(have[k, 0], j=j)
    return have


def place(grid, keys, pieces, whole_ref):
    for (k, j), piece in zip(keys, pieces):
        first = pl.multiple_of(grid.chip(k, j) * piece.shape[0], piece.shape[0])
        whole_ref[pl.ds(first, piece.shape[0]), :] = piece[...]


def early_kernel(grid, covar_ref, other_ref, errors_ref, noise_ref, order_ref, high_ref, low_ref, picked_ref):
    core = grid.here()[2]
    panel = covar_ref.shape[0]
    for at, ref in ((core, covar_ref), (1 - core, other_ref)):
        rows = pl.ds(pl.multiple_of(at * panel, panel), panel)
        high_ref[rows, :], low_ref[rows, :] = halves(ref[...])
    updates, measures = errors_ref.shape
    entry = lax.broadcasted_iota(jnp.int32, (measures, measures), 0)
    for update in range(updates):
        chosen = (entry == order_ref[update : update + 1, :]).astype(f32)
        picked_ref[update : update + 1, :] = dot(errors_ref[update : update + 1, :], chosen)
        picked_ref[updates + update : updates + update + 1, :] = dot(noise_ref[update : update + 1, :], chosen)


def product_kernel(grid, keys, high_ref, low_ref, *refs):
    pieces, (prod_ref, jac_ref) = refs[:-2], refs[-2:]
    place(grid, keys, pieces, jac_ref)
    prod_ref[...] = dot_halves((high_ref[...], low_ref[...]), halves(jac_ref[...]))


def turn_kernel(mine_ref, other_ref, high_ref, low_ref):
    m = mine_ref.shape[1]
    for at, ref in ((0, mine_ref), (m, other_ref)):
        high_ref[at : at + m, :], low_ref[at : at + m, :] = halves(ref[...].T)


def turn(mine, other):
    rows, m = mine.shape
    return call(turn_kernel, [shape(2 * m, rows, dtype=bf16)] * 2, mine, other)


def innov_kernel(grid, keys, high_ref, low_ref, *refs):
    pieces, (corr_ref, whole_ref) = refs[:-2], refs[-2:]
    place(grid, keys, pieces, whole_ref)
    m = corr_ref.shape[2]
    both = dot_halves((high_ref[...], low_ref[...]), halves(whole_ref[...]))
    corr_ref[0] = both[:m]
    corr_ref[1] = both[m:]


def tree(terms):
    while len(terms) > 1:
        terms = [sum(terms[i + 1 : i + 2], terms[i]) for i in range(0, len(terms), 2)]
    return terms[0]


def sweep(entries, count):
    get = lambda i, j: entries[max(i, j), min(i, j)]
    for p in range(count):
        inverse = 1.0 / get(p, p)
        scaled = {i: get(i, p) * inverse for i in range(count) if i != p}
        after = {}
        for i in range(count):
            for j in range(i + 1):
                if i == p and j == p:
                    after[i, j] = -inverse
                elif i == p or j == p:
                    after[i, j] = scaled[i + j - p]
                else:
                    after[i, j] = get(i, j) - scaled[i] * get(j, p)
        entries = after
    return {at: -entry for at, entry in entries.items()}


def invert(matrix):
    size = matrix.shape[0]
    lane = lax.broadcasted_iota(jnp.int32, (8, size), 1)
    sub = lax.broadcasted_iota(jnp.int32, (8, size), 0)
    spread = lambda x: jnp.broadcast_to(x, (8, size))
    groups = [matrix[at : at + 8, :] for at in range(0, size, 8)]
    for pivot in range(size // 8):
        at = 8 * pivot
        inside = (lane >= at) & (lane < at + 8)
        columns = [spread(groups[pivot][:, at + j : at + j + 1]) for j in range(8)]
        small = sweep({(i, j): spread(columns[j][i : i + 1, :]) for i in range(8) for j in range(i + 1)}, 8)
        start = jnp.where(inside, jnp.where(lane - at == sub, -1.0, 0.0), groups[pivot])
        rows = [spread(start[j : j + 1, :]) for j in range(8)]
        new = [tree([small[max(i, j), min(i, j)] * rows[j] for j in range(8)]) for i in range(8)]
        for other in range(size // 8):
            if other != pivot:
                columns = [spread(groups[other][:, at + j : at + j + 1]) for j in range(8)]
                change = tree([columns[j] * new[j] for j in range(8)])
                groups[other] = jnp.where(inside, 0.0, groups[other]) - change
        turned = new[0]
        for i in range(1, 8):
            turned = jnp.where(sub == i, new[i], turned)
        groups[pivot] = turned
    return -jnp.concatenate(groups, axis=0)


def update_kernel(grid, picked_ref, covar_ref, mine_ref, other_ref, high_ref, low_ref, *refs):
    corrs, (out_ref, step_ref) = refs[:-2], refs[-2:]
    first = grid.here()[2] == 0
    m = mine_ref.shape[1]
    panel = covar_ref.shape[0]
    diagonal = lax.broadcasted_iota(jnp.int32, (m, m), 0) == lax.broadcasted_iota(jnp.int32, (m, m), 1)
    blocks = [(corrs[i], corrs[i + 1]) for i in range(0, len(corrs), 2)]

    innov0 = jnp.where(diagonal, picked_ref[2:3, :], 0.0)
    innov1 = jnp.where(diagonal, picked_ref[3:4, :], 0.0)
    crosses = []
    for mine, other in blocks:
        innov0 = innov0 + jnp.where(first, mine[0], other[0])
        innov1 = innov1 + jnp.where(first, other[0], mine[0])
        crosses.append(jnp.where(first, mine[1], other[1]))
    inv0 = invert(innov0)
    step0 = dot(picked_ref[0:1, :], inv0)
    resid1 = picked_ref[1:2, :] - dot(step0, tree(crosses), NT)
    ratios = [dot3(cross, inv0) for cross in crosses]
    innov1 = innov1 - tree([dot3(ratio, cross, NT) for ratio, cross in zip(ratios, crosses)])
    inv1 = invert(innov1)
    step1 = dot(resid1, inv1)
    here = pl.ds(pl.multiple_of(lax.axis_index("rows") * panel, panel), panel)
    mine, other = mine_ref[here, :], other_ref[here, :]
    prod0 = jnp.where(first, mine, other)
    prod1 = jnp.where(first, other, mine) - dot3(prod0, ratios[0], NT)
    step_ref[...] = dot(step0, prod0, NT) + dot(step1, prod1, NT)
    gain1 = dot3(prod1, inv1)
    gain0 = dot3(prod0, inv0) - dot3(gain1, ratios[0])
    gain = jnp.concatenate([jnp.where(first, gain0, gain1), jnp.where(first, gain1, gain0)], axis=1)
    out_ref[...] = covar_ref[...] - dot_halves(halves(gain), (high_ref[...], low_ref[...]))


def body(sizes, covariance, jac_parts, errors, noise, order):
    blocks = sizes["blk"]
    grid = Grid(sizes["rows"])
    _, panel, size = covariance.shape
    updates, m = errors.shape
    covar = covariance.reshape(panel, size)
    chip_rows = grid.cores * panel

    terms = reduce_scatter(grid, jac_parts.reshape(updates, size, m))
    covar_other = grid.send(covar, c=1)
    high, low, picked = call(
        functools.partial(early_kernel, grid),
        [shape(chip_rows, size, dtype=bf16)] * 2 + [shape(2 * updates, m)],
        covar, covar_other, errors, noise, order,
    )
    jac_own = call(functools.partial(sum_kernel, len(terms)), [shape(chip_rows, m)], *terms)[0]
    jacs = all_gather(grid, jac_own)
    keys = list(jacs)
    prod_own, jac = call(
        functools.partial(product_kernel, grid, keys),
        [shape(chip_rows, m), shape(size, m)],
        high, low, *jacs.values(),
        flops=6 * chip_rows * size * m,
    )
    prods = all_gather(grid, prod_own)
    turned = turn(jac, grid.send(jac, c=1))
    corr, prod = call(
        functools.partial(innov_kernel, grid, keys),
        [shape(2, m, m), shape(size, m)],
        *turned, *prods.values(),
        flops=12 * m * size * m,
    )
    corrs = []
    for shift in range(blocks):
        got = lax.ppermute(corr, "blk", [(b, (b + shift) % blocks) for b in range(blocks)]) if shift else corr
        corrs += [got, grid.send(got, c=1)]
    prod_other = grid.send(prod, c=1)
    out, step = call(
        functools.partial(update_kernel, grid),
        [shape(panel, size), shape(1, panel)],
        picked, covar, prod, prod_other, *turn(prod, prod_other), *corrs,
        flops=12 * panel * m * size,
    )
    return out.reshape(covariance.shape), step


def solution(mesh):
    in_specs = (P("blk", "rows", None), P("rows", None, "blk", None, None), P(), P(), P())
    out_specs = (P("blk", "rows", None), P("blk", "rows"))
    return jax.shard_map(
        functools.partial(body, dict(mesh.shape)),
        mesh=mesh,
        in_specs=in_specs,
        out_specs=out_specs,
        check_vma=False,
    )
```
